512 devices in a mesh: section: 8 (over y_hi, core), expert: 8 (over x, y_lo), tensor: 8 (over z).
Axes of the slice: x: 4, y: 8 (y_hi: 4, y_lo: 2; y = y_hi * 2 + y_lo), z: 8, core: 2. Of those that a mesh axis runs over, the one named last changes fastest.
Arguments:
- branch_weights: bfloat16 [8, 8192, 8192], P('expert', ('section', 'tensor')), may hold values from -0.125 to 0.125
- branch_gains: float32 [8, 8192], P('expert', ('section', 'tensor')), may hold values from 0.1 to 1.9
- column_order: int32 [8, 8192], P('expert'), may hold values from 0 to 8191, each once within a row
- layer_order: int32 [4], replicated, may hold values from 0 to 3, each once
- probe_seeds: int32 [1024], replicated, may hold values from 1 to 32767
Outputs:
- expert_weights: bfloat16 [8, 8192, 8192], P('expert', None, ('section', 'tensor'))
- checksum: float32 [8, 1024, 8192], P('expert', None, ('section', 'tensor'))
- fingerprint: float32 [8, 1024], P('expert')
- shared_gain: float32 [8192], replicated
The draws below stay inside these ranges and needn't reach their ends.
Inputs may be any that keep to these rules, and one draw needn't show every extreme that they name: Each row of column_order names every hidden unit once. layer_order names every layer once.
All inputs are finite; a program needn't handle non-finite values.
Results may differ from the reference program's by a relative error of at most 0.0034.
Values may be sent and summed in bfloat16 or wider, within the bound.
No kernel may reach another device: no remote copies, remote signals or barrier semaphores. Data moves between devices by JAX's collectives and lax.ppermute only.
A program may use at most 64 MiB of HBM per device.

```python
import jax
import jax.numpy as jnp
from jax import lax

D = 2048
FF = 8192
LAYERS = 4
PROBES = 1024
EXPERTS = 8


def touch_ends(drawn, rng, least, top_value):
    index_at = [jax.random.randint(jax.random.fold_in(rng, axis), (), 0, length) for axis, length in enumerate(drawn.shape)]
    main_axis = drawn.shape.index(max(drawn.shape))
    beside = index_at[:main_axis] + [(index_at[main_axis] + 1) % drawn.shape[main_axis]] + index_at[main_axis + 1:]
    return drawn.at[tuple(index_at)].set(least).at[tuple(beside)].set(top_value)


def steps_of(key, shape, shards, least, top_value):
    factor_of = 1.0
    for dim, parts in shards:
        heights = jax.random.uniform(jax.random.fold_in(jax.random.fold_in(key, 6), dim), (parts,), jnp.float32, least / len(shards), top_value / len(shards))
        factor_of = factor_of * jnp.repeat(jnp.exp(heights), shape[dim] // parts).reshape((-1,) + (1,) * (len(shape) - 1 - dim))
    return factor_of


def scatter_about(key, dims, width, bound, split=(), kind=jnp.bfloat16):
    entries = width * jax.random.normal(key, dims, jnp.float32)
    if split:
        entries = entries * steps_of(key, dims, split, -0.22, 0.18)
    return jnp.clip(entries, -bound, bound).astype(kind)


def setup_inputs(seed: int = 0) -> dict:
    key_of = jax.random.split(jax.random.key(seed), 6)
    return {
        "branch_weights": scatter_about(key_of[0], (EXPERTS, LAYERS * D, FF), D ** -0.5, 0.125, ((0, 8), (1, 64))),
        "branch_gains": jnp.clip(1.0 + 0.18 * jax.random.normal(key_of[1], (EXPERTS, LAYERS * D), jnp.float32), 0.1, 1.9),
        "column_order": jax.vmap(lambda own: jax.random.permutation(own, FF))(jax.random.split(key_of[2], EXPERTS)).reshape((EXPERTS, FF)).astype(jnp.int32),
        "layer_order": jax.random.permutation(key_of[3], LAYERS).astype(jnp.int32),
        "probe_seeds": touch_ends(jax.random.randint(key_of[4], (PROBES,), 1, 32768), jax.random.fold_in(key_of[4], 1), 1, 32767).astype(jnp.int32),
    }


def probe_at(probe_seeds, row_ids):
    hashed = (probe_seeds[:, None] * (row_ids[None, :] + 1)) % 65521
    return ((hashed % 511) - 255).astype(jnp.float32) / 256.0


def reference(branch_weights, branch_gains, column_order, layer_order, probe_seeds):
    mean_gain = jnp.sum(branch_gains, axis=0) / EXPERTS
    slot_ids = jnp.arange(LAYERS, dtype=jnp.int32)
    inverse = jnp.sum(jnp.where(layer_order[None, :] == slot_ids[:, None], slot_ids[None, :], 0), axis=1).astype(jnp.int32)
    shared_gain = mean_gain.reshape(LAYERS, D)[inverse].reshape(LAYERS * D)
    probes = probe_at(probe_seeds, jnp.arange(LAYERS * D, dtype=jnp.int32)).astype(jnp.bfloat16)
    seven = jnp.full((1,), 7919, jnp.int32)
    column_probe = probe_at(seven, jnp.arange(FF, dtype=jnp.int32))[0]

    def one_expert(inputs):
        weights, own_gains, order = inputs
        permuted = jnp.take(weights, order, axis=1)
        scaling = own_gains / mean_gain
        folded = (permuted.astype(jnp.float32) * scaling[:, None]).astype(jnp.bfloat16)
        natural = folded.reshape(LAYERS, D, FF)[inverse].reshape(LAYERS * D, FF)
        sketches = jnp.dot(probes, natural, preferred_element_type=jnp.float32)
        printed = jnp.dot(sketches, column_probe, precision=lax.Precision.HIGHEST) * (FF ** -0.5)
        return natural, sketches, printed

    expert_weights, checksum, fingerprint = lax.map(one_expert, (branch_weights, branch_gains, column_order))
    return expert_weights, checksum, fingerprint, shared_gain
```

```python
import functools

import jax
import jax.numpy as jnp
import numpy as np
from jax import lax
from jax.experimental import pallas as pl
from jax.experimental.pallas import tpu as pltpu
from jax.sharding import PartitionSpec as P

D = 2048
FF = 8192
LAYERS = 4
PROBES = 1024
ROWS = 128
COLS = 128
GROUPS = 64
SENT = ROWS + 8
PRIME = 65521
STACK = ("section", "tensor")
MIB = 1 << 20

VMEM = pl.BlockSpec(memory_space=pltpu.VMEM)
SMEM = pl.BlockSpec(memory_space=pltpu.SMEM)
ANY = pl.BlockSpec(memory_space=pl.ANY)


def column_probe():
    hashed = (7919 * (np.arange(FF, dtype=np.int64) + 1)) % PRIME
    return ((hashed % 511 - 255) / 256.0).astype(np.float32).reshape(GROUPS, COLS)


def turn_kernel(w_ref, t_ref):
    def step(s, _):
        at = pl.multiple_of(s * 128, 128)
        t_ref[pl.ds(at, 128), :] = w_ref[:, pl.ds(at, 128)].T.astype(jnp.float32)
        return 0

    lax.fori_loop(0, FF // 128, step, 0, unroll=4)


def turn(weights):
    return pl.pallas_call(
        turn_kernel,
        out_shape=jax.ShapeDtypeStruct((FF, ROWS), jnp.float32),
        in_specs=[VMEM],
        out_specs=VMEM,
        compiler_params=pltpu.CompilerParams(vmem_limit_bytes=8 * MIB),
        cost_estimate=pl.CostEstimate(flops=0, bytes_accessed=6 * MIB, transcendentals=0),
        name="turn",
    )(weights)


def pieces(value):
    high = value.astype(jnp.bfloat16).astype(jnp.float32)
    rest = value - high
    middle = rest.astype(jnp.bfloat16).astype(jnp.float32)
    return [high, middle, rest - middle]


def pick_kernel(order_ref, t_ref, gains_ref, own_ref, probe_ref, out_ref, held, sem, *, per):
    mean = jnp.sum(gains_ref[...], axis=0, keepdims=True) * (1.0 / 8.0)
    scale = own_ref[...] / mean
    sublane = lax.broadcasted_iota(jnp.int32, (8, 128), 0)
    masks = [sublane == i for i in range(8)]

    def block(d):
        tiles = []
        for j in range(0, COLS, 8):
            tile = t_ref[pl.ds(order_ref[d * COLS + j], 8, stride=0), :]
            for i in range(1, 8):
                row = t_ref[pl.ds(order_ref[d * COLS + j + i], 8, stride=0), :]
                tile = jnp.where(masks[i], row, tile)
            tiles.append(tile)
        return jnp.concatenate(tiles, axis=0)

    def step(p, total):
        picked = [block(p * per + q) for q in range(per)]
        for q in range(per):
            d = p * per + q
            folded = (picked[q] * scale).astype(jnp.bfloat16).T
            held[d, 0:ROWS, :] = folded
            total = total + folded.astype(jnp.float32) * probe_ref[pl.ds(d, 1), :]
        return total

    total = lax.fori_loop(0, GROUPS // per, step, jnp.zeros((ROWS, COLS), jnp.float32))
    printed = jnp.sum(total.T, axis=0, keepdims=True)
    rows = pieces(printed) + pieces(mean) + [jnp.zeros((2, 128), jnp.float32)]
    extra = jnp.concatenate(rows, axis=0).astype(jnp.bfloat16)

    def fill(d, _):
        held[d, ROWS:SENT, :] = extra
        return 0

    lax.fori_loop(0, GROUPS, fill, 0, unroll=8)
    copy = pltpu.make_async_copy(held, out_ref, sem)
    copy.start()
    copy.wait()


def pick(order, turned, gains, own):
    return pl.pallas_call(
        functools.partial(pick_kernel, per=4),
        out_shape=jax.ShapeDtypeStruct((GROUPS, SENT, COLS), jnp.bfloat16),
        in_specs=[SMEM, VMEM, VMEM, VMEM, VMEM],
        out_specs=ANY,
        scratch_shapes=[
            pltpu.VMEM((GROUPS, SENT, COLS), jnp.bfloat16),
            pltpu.SemaphoreType.DMA,
        ],
        compiler_params=pltpu.CompilerParams(vmem_limit_bytes=8 * MIB),
        cost_estimate=pl.CostEstimate(flops=0, bytes_accessed=24 * MIB, transcendentals=0),
        name="pick",
    )(order, turned, gains, own, column_probe())


def reduced(value):
    left = value - (value.astype(jnp.float32) * (1.0 / PRIME)).astype(jnp.int32) * PRIME
    left = jnp.where(left < 0, left + PRIME, left)
    return jnp.where(left >= PRIME, left - PRIME, left)


def probes_kernel(layer_ref, seeds_ref, out_ref):
    lane = lax.broadcasted_iota(jnp.int32, (8, 128), 1)

    def rows(j, _):
        at = pl.multiple_of(j * 16, 16)
        seeds = [jnp.broadcast_to(seeds_ref[pl.ds(at + 8 * u, 8), :], (8, 128)) for u in range(2)]
        steps = [reduced(seed * 128) for seed in seeds]
        for b in range(LAYERS):
            hashed = [reduced(seed * (layer_ref[b] * D + 1 + lane)) for seed in seeds]
            for c in range(0, D, 128):
                made = []
                for u in range(2):
                    value = hashed[u]
                    small = lax.shift_right_logical(value, 9) + (value & 511)
                    small = jnp.where(small >= 511, small - (511 + 255), small - 255)
                    made.append(small.astype(jnp.float32) * (1.0 / 256.0))
                    after = value + steps[u] - PRIME
                    hashed[u] = jnp.where(after < 0, after + PRIME, after)
                out_ref[pl.ds(at, 16), b * D + c : b * D + c + 128] = jnp.concatenate(
                    made, axis=0
                ).astype(jnp.bfloat16)
        return 0

    lax.fori_loop(0, PROBES // 16, rows, 0)


def make_probes(layer_order, seeds):
    return pl.pallas_call(
        probes_kernel,
        out_shape=jax.ShapeDtypeStruct((PROBES, LAYERS * D), jnp.bfloat16),
        in_specs=[SMEM, VMEM],
        out_specs=VMEM,
        compiler_params=pltpu.CompilerParams(vmem_limit_bytes=8 * MIB),
        cost_estimate=pl.CostEstimate(flops=0, bytes_accessed=64 * MIB, transcendentals=0),
        name="probes",
    )(layer_order, seeds.reshape(PROBES, 1))


def sketch_kernel(
    layer_ref, in_ref, probes_ref, out_ref, sums_ref, print_ref, gain_ref, total, turned, sem
):
    per_layer = GROUPS // LAYERS

    def placed(b):
        return pltpu.make_async_copy(
            in_ref.at[pl.ds(per_layer * b, per_layer), pl.ds(0, ROWS), :],
            out_ref.at[pl.ds(layer_ref[b] * per_layer, per_layer)],
            sem,
        )

    for b in range(LAYERS):
        placed(b).start()
    extra = in_ref[:, ROWS:SENT, :].astype(jnp.float32)
    mean = extra[:, 3, :] + extra[:, 4, :] + extra[:, 5, :]
    for b in range(LAYERS):
        at = pl.multiple_of(layer_ref[b] * per_layer, per_layer)
        gain_ref[pl.ds(at, per_layer), :] = mean[per_layer * b : per_layer * (b + 1)]
    row = lax.broadcasted_iota(jnp.int32, extra.shape, 1)
    printed = jnp.where(row < 3, extra, 0.0).reshape(GROUPS * 8, ROWS)
    for j in range(4):
        turned[j] = printed[j * 128 : (j + 1) * 128].T
    lane = lax.broadcasted_iota(jnp.int32, (ROWS, 128), 1) // 8

    for b in range(LAYERS):
        blocks = []
        for g in range(per_layer):
            beside = jnp.where(lane == g, turned[b], 0.0).astype(jnp.bfloat16)
            blocks.append(jnp.concatenate([in_ref[b * per_layer + g, 0:ROWS, :], beside], axis=1))
        product = jnp.dot(
            probes_ref[:, b * D : (b + 1) * D],
            jnp.concatenate(blocks, axis=0),
            preferred_element_type=jnp.float32,
        )
        if b == 0:
            total[...] = product
        else:
            total[...] += product
    sums_ref[...] = total[:, 0:COLS]
    for j in range(PROBES // 128):
        part = total[j * 128 : (j + 1) * 128, COLS:].T
        print_ref[:, j * 128 : (j + 1) * 128] = jnp.sum(part, axis=0, keepdims=True) * FF ** (-0.5)
    for b in range(LAYERS):
        placed(b).wait()


def sketch(layer_order, arrived, probes):
    return pl.pallas_call(
        sketch_kernel,
        out_shape=(
            jax.ShapeDtypeStruct((GROUPS, ROWS, COLS), jnp.bfloat16),
            jax.ShapeDtypeStruct((PROBES, COLS), jnp.float32),
            jax.ShapeDtypeStruct((1, PROBES), jnp.float32),
            jax.ShapeDtypeStruct((GROUPS, ROWS), jnp.float32),
        ),
        in_specs=[SMEM, VMEM, VMEM],
        out_specs=(ANY, VMEM, VMEM, VMEM),
        scratch_shapes=[
            pltpu.VMEM((PROBES, 256), jnp.float32),
            pltpu.VMEM((4, ROWS, 128), jnp.float32),
            pltpu.SemaphoreType.DMA,
        ],
        compiler_params=pltpu.CompilerParams(vmem_limit_bytes=12 * MIB),
        cost_estimate=pl.CostEstimate(
            flops=2 * PROBES * LAYERS * D * COLS, bytes_accessed=22 * MIB, transcendentals=0
        ),
        name="sketch",
    )(layer_order, arrived, probes)


def local(branch_weights, branch_gains, column_order, layer_order, probe_seeds):
    gains = lax.all_to_all(
        jnp.broadcast_to(branch_gains[None], (8, 1, ROWS)), "expert", 0, 0, tiled=True
    ).reshape(8, ROWS)
    turned = turn(branch_weights[0])
    blocks = pick(column_order[0], turned, gains, branch_gains)
    blocks, seeds = lax.optimization_barrier((blocks, probe_seeds))
    arrived = lax.all_to_all(blocks, STACK, 0, 0, tiled=True)
    probes = make_probes(layer_order, seeds)
    ordered, sums, printed, shared = sketch(layer_order, arrived, probes)
    return (
        ordered.reshape(1, LAYERS * D, COLS),
        sums[None],
        printed.reshape(1, PROBES),
        shared.reshape(LAYERS * D),
    )


def solution(mesh):
    return jax.shard_map(
        local,
        mesh=mesh,
        in_specs=(
            P("expert", STACK, None),
            P("expert", STACK),
            P("expert", None),
            P(),
            P(),
        ),
        out_specs=(
            P("expert", None, STACK),
            P("expert", None, STACK),
            P("expert", None),
            P(),
        ),
        check_vma=False,
    )
```

```python
import functools

import jax
import jax.numpy as jnp
import numpy as np
from jax import lax
from jax.experimental import pallas as pl
from jax.experimental.pallas import tpu as pltpu
from jax.sharding import PartitionSpec as P

D = 2048
FF = 8192
LAYERS = 4
PROBES = 1024
ROWS = 128
COLS = 128
GROUPS = 64
SENT = ROWS + 8
PRIME = 65521
STACK = ("section", "tensor")
MIB = 1 << 20

VMEM = pl.BlockSpec(memory_space=pltpu.VMEM)
SMEM = pl.BlockSpec(memory_space=pltpu.SMEM)
ANY = pl.BlockSpec(memory_space=pl.ANY)


def column_probe():
    hashed = (7919 * (np.arange(FF, dtype=np.int64) + 1)) % PRIME
    return ((hashed % 511 - 255) / 256.0).astype(np.float32).reshape(GROUPS, COLS)


def gather_kernel(
    order_ref, w_ref, out_ref, packed, pairs, rows, turned, held, sem, in_sem, out_sem
):
    parts = 4
    wide = FF // parts

    def fetch(c):
        at = pl.ds(c * wide, wide)
        return pltpu.make_async_copy(w_ref.at[:, at], rows.at[:, at], in_sem.at[c])

    for c in range(parts):
        fetch(c).start()
    half = GROUPS // 2
    packed[...] = order_ref[0:half, :] + order_ref[half:, :] * 65536
    copy = pltpu.make_async_copy(packed, pairs, sem)
    copy.start()
    for c in range(parts):
        fetch(c).wait()

        def turn(s, _):
            at = pl.multiple_of(c * wide + s * 128, 128)
            turned[pl.ds(at, 128), :] = rows[:, pl.ds(at, 128)].T.astype(jnp.float32)
            return 0

        lax.fori_loop(0, wide // 128, turn, 0, unroll=4)
    copy.wait()
    sublane = lax.broadcasted_iota(jnp.int32, (8, 128), 0)
    masks = [sublane == i for i in range(8)]

    def send(at, count):
        return pltpu.make_async_copy(
            held.at[pl.ds(at, count)], out_ref.at[pl.ds(at, count)], out_sem
        )

    def both(p):
        tiles = ([], [])
        for j in range(0, COLS, 8):
            made = [None, None]
            for i in range(8):
                word = pairs[p, j + i]
                for u, column in enumerate((word & 65535, lax.shift_right_logical(word, 16))):
                    row = turned[pl.ds(column, 8, stride=0), :]
                    made[u] = row if i == 0 else jnp.where(masks[i], row, made[u])
            for u in range(2):
                tiles[u].append(made[u])
        for u in range(2):
            held[p + half * u] = jnp.concatenate(tiles[u], axis=0).astype(jnp.bfloat16).T

    def step(s, _):
        for q in range(4):
            both(s * 4 + q)
        send(s * 4, 4).start()
        send(s * 4 + half, 4).start()
        return 0

    lax.fori_loop(0, half // 4, step, 0)
    send(0, GROUPS).wait()


def gather(order, weights):
    return pl.pallas_call(
        gather_kernel,
        out_shape=jax.ShapeDtypeStruct((GROUPS, ROWS, COLS), jnp.bfloat16),
        in_specs=[VMEM, ANY],
        out_specs=ANY,
        scratch_shapes=[
            pltpu.VMEM((GROUPS // 2, COLS), jnp.int32),
            pltpu.SMEM((GROUPS // 2, COLS), jnp.int32),
            pltpu.VMEM((ROWS, FF), jnp.bfloat16),
            pltpu.VMEM((FF, ROWS), jnp.float32),
            pltpu.VMEM((GROUPS, ROWS, COLS), jnp.bfloat16),
            pltpu.SemaphoreType.DMA,
            pltpu.SemaphoreType.DMA((4,)),
            pltpu.SemaphoreType.DMA,
        ],
        compiler_params=pltpu.CompilerParams(vmem_limit_bytes=59 * MIB),
        cost_estimate=pl.CostEstimate(flops=0, bytes_accessed=24 * MIB, transcendentals=0),
        name="gather",
    )(order.reshape(GROUPS, COLS), weights)


def pieces(value):
    high = value.astype(jnp.bfloat16).astype(jnp.float32)
    rest = value - high
    middle = rest.astype(jnp.bfloat16).astype(jnp.float32)
    return [high, middle, rest - middle]


def fold_kernel(raw_ref, gains_ref, own_ref, probe_ref, out_ref, rows, held, extra, in_sem, sem):
    parts, count = 4, GROUPS // 4

    def fetch(c):
        at = pl.ds(c * count, count)
        return pltpu.make_async_copy(raw_ref.at[at], rows.at[at], in_sem.at[c])

    def send(c):
        at = pl.ds(c * count, count)
        return pltpu.make_async_copy(held.at[at], out_ref.at[at, pl.ds(0, ROWS), :], sem.at[c])

    for c in range(parts):
        fetch(c).start()
    mean = jnp.sum(gains_ref[...], axis=0, keepdims=True) * (1.0 / 8.0)
    scale = jnp.broadcast_to(own_ref[...] / mean, (COLS, ROWS)).T
    total = jnp.zeros((ROWS, COLS), jnp.float32)
    for c in range(parts):
        fetch(c).wait()

        def step(s, total):
            d = c * count + s
            folded = (rows[d].astype(jnp.float32) * scale).astype(jnp.bfloat16)
            held[d] = folded
            return total + folded.astype(jnp.float32) * probe_ref[pl.ds(d, 1), :]

        total = lax.fori_loop(0, count, step, total, unroll=4)
        send(c).start()
    printed = jnp.sum(total.T, axis=0, keepdims=True)
    added = pieces(printed) + pieces(mean) + [jnp.zeros((2, ROWS), jnp.float32)]
    added = jnp.concatenate(added, axis=0).astype(jnp.bfloat16)
    extra[...] = jnp.broadcast_to(added[None], extra.shape)
    copy = pltpu.make_async_copy(extra, out_ref.at[:, pl.ds(ROWS, SENT - ROWS), :], sem.at[parts])
    copy.start()
    for c in range(parts):
        send(c).wait()
    copy.wait()


def fold(raw, gains, own):
    return pl.pallas_call(
        fold_kernel,
        out_shape=jax.ShapeDtypeStruct((GROUPS, SENT, COLS), jnp.bfloat16),
        in_specs=[ANY, VMEM, VMEM, VMEM],
        out_specs=ANY,
        scratch_shapes=[
            pltpu.VMEM((GROUPS, ROWS, COLS), jnp.bfloat16),
            pltpu.VMEM((GROUPS, ROWS, COLS), jnp.bfloat16),
            pltpu.VMEM((GROUPS, SENT - ROWS, COLS), jnp.bfloat16),
            pltpu.SemaphoreType.DMA((4,)),
            pltpu.SemaphoreType.DMA((5,)),
        ],
        compiler_params=pltpu.CompilerParams(vmem_limit_bytes=59 * MIB),
        cost_estimate=pl.CostEstimate(flops=0, bytes_accessed=5 * MIB, transcendentals=0),
        name="fold",
    )(raw, gains, own, column_probe())


def reduced(value):
    left = value - (value.astype(jnp.float32) * (1.0 / PRIME)).astype(jnp.int32) * PRIME
    left = jnp.where(left < 0, left + PRIME, left)
    return jnp.where(left >= PRIME, left - PRIME, left)


def probes_kernel(layer_ref, seeds_ref, out_ref):
    lane = lax.broadcasted_iota(jnp.int32, (8, 128), 1)

    def rows(j, _):
        at = pl.multiple_of(j * 16, 16)
        seeds = [jnp.broadcast_to(seeds_ref[pl.ds(at + 8 * u, 8), :], (8, 128)) for u in range(2)]
        steps = [reduced(seed * 128) for seed in seeds]
        for b in range(LAYERS):
            hashed = [reduced(seed * (layer_ref[b] * D + 1 + lane)) for seed in seeds]
            for c in range(0, D, 128):
                made = []
                for u in range(2):
                    value = hashed[u]
                    small = lax.shift_right_logical(value, 9) + (value & 511)
                    small = jnp.where(small >= 511, small - (511 + 255), small - 255)
                    made.append(small.astype(jnp.float32) * (1.0 / 256.0))
                    after = value + steps[u] - PRIME
                    hashed[u] = jnp.where(after < 0, after + PRIME, after)
                out_ref[pl.ds(at, 16), b * D + c : b * D + c + 128] = jnp.concatenate(
                    made, axis=0
                ).astype(jnp.bfloat16)
        return 0

    lax.fori_loop(0, out_ref.shape[0] // 16, rows, 0)


def make_probes(layer_order, seeds):
    rows = PROBES // 8
    return pl.pallas_call(
        probes_kernel,
        out_shape=jax.ShapeDtypeStruct((PROBES, LAYERS * D), jnp.bfloat16),
        grid_spec=pltpu.PrefetchScalarGridSpec(
            num_scalar_prefetch=1,
            grid=(8,),
            in_specs=[pl.BlockSpec((rows, 1), lambda j, order: (j, 0))],
            out_specs=pl.BlockSpec((rows, LAYERS * D), lambda j, order: (j, 0)),
        ),
        compiler_params=pltpu.CompilerParams(vmem_limit_bytes=56 * MIB),
        cost_estimate=pl.CostEstimate(flops=0, bytes_accessed=64 * MIB, transcendentals=0),
        name="probes",
    )(layer_order, seeds.reshape(PROBES, 1))


def sketch_kernel(
    layer_ref, in_ref, probes_ref, out_ref, sums_ref, print_ref, gain_ref, total, turned, sem
):
    per_layer = GROUPS // LAYERS

    def placed(b):
        return pltpu.make_async_copy(
            in_ref.at[pl.ds(per_layer * b, per_layer), pl.ds(0, ROWS), :],
            out_ref.at[pl.ds(layer_ref[b] * per_layer, per_layer)],
            sem,
        )

    for b in range(LAYERS):
        placed(b).start()
    extra = in_ref[:, ROWS:SENT, :].astype(jnp.float32)
    mean = extra[:, 3, :] + extra[:, 4, :] + extra[:, 5, :]
    for b in range(LAYERS):
        at = pl.multiple_of(layer_ref[b] * per_layer, per_layer)
        gain_ref[pl.ds(at, per_layer), :] = mean[per_layer * b : per_layer * (b + 1)]
    row = lax.broadcasted_iota(jnp.int32, extra.shape, 1)
    printed = jnp.where(row < 3, extra, 0.0).reshape(GROUPS * 8, ROWS)
    for j in range(4):
        turned[j] = printed[j * 128 : (j + 1) * 128].T
    lane = lax.broadcasted_iota(jnp.int32, (ROWS, 128), 1) // 8

    for b in range(LAYERS):
        blocks = []
        for g in range(per_layer):
            beside = jnp.where(lane == g, turned[b], 0.0).astype(jnp.bfloat16)
            blocks.append(jnp.concatenate([in_ref[b * per_layer + g, 0:ROWS, :], beside], axis=1))
        product = jnp.dot(
            probes_ref[:, b * D : (b + 1) * D],
            jnp.concatenate(blocks, axis=0),
            preferred_element_type=jnp.float32,
        )
        if b == 0:
            total[...] = product
        else:
            total[...] += product
    sums_ref[...] = total[:, 0:COLS]
    for j in range(PROBES // 128):
        part = total[j * 128 : (j + 1) * 128, COLS:].T
        print_ref[:, j * 128 : (j + 1) * 128] = jnp.sum(part, axis=0, keepdims=True) * FF ** (-0.5)
    for b in range(LAYERS):
        placed(b).wait()


def sketch(layer_order, arrived, probes):
    return pl.pallas_call(
        sketch_kernel,
        out_shape=(
            jax.ShapeDtypeStruct((GROUPS, ROWS, COLS), jnp.bfloat16),
            jax.ShapeDtypeStruct((PROBES, COLS), jnp.float32),
            jax.ShapeDtypeStruct((1, PROBES), jnp.float32),
            jax.ShapeDtypeStruct((GROUPS, ROWS), jnp.float32),
        ),
        in_specs=[SMEM, VMEM, VMEM],
        out_specs=(ANY, VMEM, VMEM, VMEM),
        scratch_shapes=[
            pltpu.VMEM((PROBES, 256), jnp.float32),
            pltpu.VMEM((4, ROWS, 128), jnp.float32),
            pltpu.SemaphoreType.DMA,
        ],
        compiler_params=pltpu.CompilerParams(vmem_limit_bytes=12 * MIB),
        cost_estimate=pl.CostEstimate(
            flops=2 * PROBES * LAYERS * D * COLS, bytes_accessed=22 * MIB, transcendentals=0
        ),
        name="sketch",
    )(layer_order, arrived, probes)


def local(branch_weights, branch_gains, column_order, layer_order, probe_seeds):
    gains = lax.all_to_all(
        jnp.broadcast_to(branch_gains[None], (8, 1, ROWS)), "expert", 0, 0, tiled=True
    ).reshape(8, ROWS)
    raw = gather(column_order[0], branch_weights[0])
    blocks = fold(raw, gains, branch_gains)
    blocks, seeds = lax.optimization_barrier((blocks, probe_seeds))
    arrived = lax.all_to_all(blocks, STACK, 0, 0, tiled=True)
    probes = make_probes(layer_order, seeds)
    ordered, sums, printed, shared = sketch(layer_order, arrived, probes)
    return (
        ordered.reshape(1, LAYERS * D, COLS),
        sums[None],
        printed.reshape(1, PROBES),
        shared.reshape(LAYERS * D),
    )


def solution(mesh):
    return jax.shard_map(
        local,
        mesh=mesh,
        in_specs=(
            P("expert", STACK, None),
            P("expert", STACK),
            P("expert", None),
            P(),
            P(),
        ),
        out_specs=(
            P("expert", None, STACK),
            P("expert", None, STACK),
            P("expert", None),
            P(),
        ),
        check_vma=False,
    )
```

```python
import functools

import jax
import jax.numpy as jnp
import numpy as np
from jax import lax
from jax.experimental import pallas as pl
from jax.experimental.pallas import tpu as pltpu
from jax.sharding import PartitionSpec as P

D = 2048
FF = 8192
LAYERS = 4
PROBES = 1024
ROWS = 128
COLS = 128
GROUPS = 64
SENT = ROWS + 8
PRIME = 65521
STACK = ("section", "tensor")
MIB = 1 << 20

VMEM = pl.BlockSpec(memory_space=pltpu.VMEM)
SMEM = pl.BlockSpec(memory_space=pltpu.SMEM)
ANY = pl.BlockSpec(memory_space=pl.ANY)


def column_probe():
    hashed = (7919 * (np.arange(FF, dtype=np.int64) + 1)) % PRIME
    return ((hashed % 511 - 255) / 256.0).astype(np.float32).reshape(GROUPS, COLS)


def gather_kernel(order_ref, w_ref, out_ref, order, packed, pairs, turned, held, sem, out_sem):
    half = GROUPS // 2
    fetch = pltpu.make_async_copy(order_ref, order, sem.at[0])
    fetch.start()

    def turn(s, _):
        at = pl.multiple_of(s * 128, 128)
        turned[pl.ds(at, 128), :] = w_ref[:, pl.ds(at, 128)].T.astype(jnp.float32)
        return 0

    lax.fori_loop(0, FF // 256, turn, 0, unroll=16)
    fetch.wait()
    packed[...] = order[0:half, :] + order[half:, :] * 65536
    copy = pltpu.make_async_copy(packed, pairs, sem.at[1])
    copy.start()
    lax.fori_loop(FF // 256, FF // 128, turn, 0, unroll=16)
    copy.wait()
    sublane = lax.broadcasted_iota(jnp.int32, (8, 128), 0)
    masks = [sublane == i for i in range(8)]

    def send(at, count):
        return pltpu.make_async_copy(
            held.at[pl.ds(at, count)], out_ref.at[pl.ds(at, count)], out_sem
        )

    def both(p):
        tiles = ([], [])
        for j in range(0, COLS, 8):
            made = [None, None]
            for i in range(8):
                word = pairs[p, j + i]
                for u, column in enumerate((word & 65535, lax.shift_right_logical(word, 16))):
                    row = turned[pl.ds(column, 8, stride=0), :]
                    made[u] = row if i == 0 else jnp.where(masks[i], row, made[u])
            for u in range(2):
                tiles[u].append(made[u])
        for u in range(2):
            held[p + half * u] = jnp.concatenate(tiles[u], axis=0).astype(jnp.bfloat16).T

    def step(s, _):
        for q in range(8):
            both(s * 8 + q)
        send(s * 8, 8).start()
        send(s * 8 + half, 8).start()
        return 0

    lax.fori_loop(0, half // 8, step, 0)
    send(0, GROUPS).wait()


def gather(order, weights):
    return pl.pallas_call(
        gather_kernel,
        out_shape=jax.ShapeDtypeStruct((GROUPS, ROWS, COLS), jnp.bfloat16),
        in_specs=[ANY, VMEM],
        out_specs=ANY,
        scratch_shapes=[
            pltpu.VMEM((GROUPS, COLS), jnp.int32),
            pltpu.VMEM((GROUPS // 2, COLS), jnp.int32),
            pltpu.SMEM((GROUPS // 2, COLS), jnp.int32),
            pltpu.VMEM((FF, ROWS), jnp.float32),
            pltpu.VMEM((GROUPS, ROWS, COLS), jnp.bfloat16),
            pltpu.SemaphoreType.DMA((2,)),
            pltpu.SemaphoreType.DMA,
        ],
        compiler_params=pltpu.CompilerParams(vmem_limit_bytes=12 * MIB),
        cost_estimate=pl.CostEstimate(flops=0, bytes_accessed=24 * MIB, transcendentals=0),
        name="gather",
    )(order.reshape(GROUPS, COLS), weights)


def pieces(value):
    high = value.astype(jnp.bfloat16).astype(jnp.float32)
    rest = value - high
    middle = rest.astype(jnp.bfloat16).astype(jnp.float32)
    return [high, middle, rest - middle]


def fold_kernel(raw_ref, gains_ref, own_ref, probe_ref, out_ref, held, extra, sem):
    mean = jnp.sum(gains_ref[...], axis=0, keepdims=True) * (1.0 / 8.0)
    scale = jnp.broadcast_to(own_ref[...] / mean, (COLS, ROWS)).T
    parts, count = 4, GROUPS // 4

    def send(c):
        return pltpu.make_async_copy(
            held.at[pl.ds(c * count, count)],
            out_ref.at[pl.ds(c * count, count), pl.ds(0, ROWS), :],
            sem.at[c],
        )

    total = jnp.zeros((ROWS, COLS), jnp.float32)
    for c in range(parts):

        def step(s, total):
            d = c * count + s
            folded = (raw_ref[d].astype(jnp.float32) * scale).astype(jnp.bfloat16)
            held[d] = folded
            return total + folded.astype(jnp.float32) * probe_ref[pl.ds(d, 1), :]

        total = lax.fori_loop(0, count, step, total, unroll=4)
        send(c).start()
    printed = jnp.sum(total.T, axis=0, keepdims=True)
    rows = pieces(printed) + pieces(mean) + [jnp.zeros((2, ROWS), jnp.float32)]
    rows = jnp.concatenate(rows, axis=0).astype(jnp.bfloat16)
    extra[...] = jnp.broadcast_to(rows[None], extra.shape)
    copy = pltpu.make_async_copy(extra, out_ref.at[:, pl.ds(ROWS, SENT - ROWS), :], sem.at[parts])
    copy.start()
    for c in range(parts):
        send(c).wait()
    copy.wait()


def fold(raw, gains, own):
    return pl.pallas_call(
        fold_kernel,
        out_shape=jax.ShapeDtypeStruct((GROUPS, SENT, COLS), jnp.bfloat16),
        in_specs=[VMEM, VMEM, VMEM, VMEM],
        out_specs=ANY,
        scratch_shapes=[
            pltpu.VMEM((GROUPS, ROWS, COLS), jnp.bfloat16),
            pltpu.VMEM((GROUPS, SENT - ROWS, COLS), jnp.bfloat16),
            pltpu.SemaphoreType.DMA((5,)),
        ],
        compiler_params=pltpu.CompilerParams(vmem_limit_bytes=8 * MIB),
        cost_estimate=pl.CostEstimate(flops=0, bytes_accessed=5 * MIB, transcendentals=0),
        name="fold",
    )(raw, gains, own, column_probe())


def reduced(value):
    left = value - (value.astype(jnp.float32) * (1.0 / PRIME)).astype(jnp.int32) * PRIME
    left = jnp.where(left < 0, left + PRIME, left)
    return jnp.where(left >= PRIME, left - PRIME, left)


def probes_kernel(layer_ref, seeds_ref, out_ref):
    lane = lax.broadcasted_iota(jnp.int32, (8, 128), 1)

    def rows(j, _):
        at = pl.multiple_of(j * 16, 16)
        seeds = [jnp.broadcast_to(seeds_ref[pl.ds(at + 8 * u, 8), :], (8, 128)) for u in range(2)]
        steps = [reduced(seed * 128) for seed in seeds]
        for b in range(LAYERS):
            hashed = [reduced(seed * (layer_ref[b] * D + 1 + lane)) for seed in seeds]
            for c in range(0, D, 128):
                made = []
                for u in range(2):
                    value = hashed[u]
                    small = lax.shift_right_logical(value, 9) + (value & 511)
                    small = jnp.where(small >= 511, small - (511 + 255), small - 255)
                    made.append(small.astype(jnp.float32) * (1.0 / 256.0))
                    after = value + steps[u] - PRIME
                    hashed[u] = jnp.where(after < 0, after + PRIME, after)
                out_ref[pl.ds(at, 16), b * D + c : b * D + c + 128] = jnp.concatenate(
                    made, axis=0
                ).astype(jnp.bfloat16)
        return 0

    lax.fori_loop(0, out_ref.shape[0] // 16, rows, 0)


def make_probes(layer_order, seeds):
    rows = PROBES // 8
    return pl.pallas_call(
        probes_kernel,
        out_shape=jax.ShapeDtypeStruct((PROBES, LAYERS * D), jnp.bfloat16),
        grid_spec=pltpu.PrefetchScalarGridSpec(
            num_scalar_prefetch=1,
            grid=(8,),
            in_specs=[pl.BlockSpec((rows, 1), lambda j, order: (j, 0))],
            out_specs=pl.BlockSpec((rows, LAYERS * D), lambda j, order: (j, 0)),
        ),
        compiler_params=pltpu.CompilerParams(vmem_limit_bytes=56 * MIB),
        cost_estimate=pl.CostEstimate(flops=0, bytes_accessed=64 * MIB, transcendentals=0),
        name="probes",
    )(layer_order, seeds.reshape(PROBES, 1))


def sketch_kernel(
    layer_ref, in_ref, probes_ref, out_ref, sums_ref, print_ref, gain_ref, total, turned, sem
):
    per_layer = GROUPS // LAYERS

    def placed(b):
        return pltpu.make_async_copy(
            in_ref.at[pl.ds(per_layer * b, per_layer), pl.ds(0, ROWS), :],
            out_ref.at[pl.ds(layer_ref[b] * per_layer, per_layer)],
            sem,
        )

    for b in range(LAYERS):
        placed(b).start()
    extra = in_ref[:, ROWS:SENT, :].astype(jnp.float32)
    mean = extra[:, 3, :] + extra[:, 4, :] + extra[:, 5, :]
    for b in range(LAYERS):
        at = pl.multiple_of(layer_ref[b] * per_layer, per_layer)
        gain_ref[pl.ds(at, per_layer), :] = mean[per_layer * b : per_layer * (b + 1)]
    row = lax.broadcasted_iota(jnp.int32, extra.shape, 1)
    printed = jnp.where(row < 3, extra, 0.0).reshape(GROUPS * 8, ROWS)
    for j in range(4):
        turned[j] = printed[j * 128 : (j + 1) * 128].T
    lane = lax.broadcasted_iota(jnp.int32, (ROWS, 128), 1) // 8

    for b in range(LAYERS):
        blocks = []
        for g in range(per_layer):
            beside = jnp.where(lane == g, turned[b], 0.0).astype(jnp.bfloat16)
            blocks.append(jnp.concatenate([in_ref[b * per_layer + g, 0:ROWS, :], beside], axis=1))
        product = jnp.dot(
            probes_ref[:, b * D : (b + 1) * D],
            jnp.concatenate(blocks, axis=0),
            preferred_element_type=jnp.float32,
        )
        if b == 0:
            total[...] = product
        else:
            total[...] += product
    sums_ref[...] = total[:, 0:COLS]
    for j in range(PROBES // 128):
        part = total[j * 128 : (j + 1) * 128, COLS:].T
        print_ref[:, j * 128 : (j + 1) * 128] = jnp.sum(part, axis=0, keepdims=True) * FF ** (-0.5)
    for b in range(LAYERS):
        placed(b).wait()


def sketch(layer_order, arrived, probes):
    return pl.pallas_call(
        sketch_kernel,
        out_shape=(
            jax.ShapeDtypeStruct((GROUPS, ROWS, COLS), jnp.bfloat16),
            jax.ShapeDtypeStruct((PROBES, COLS), jnp.float32),
            jax.ShapeDtypeStruct((1, PROBES), jnp.float32),
            jax.ShapeDtypeStruct((GROUPS, ROWS), jnp.float32),
        ),
        in_specs=[SMEM, VMEM, VMEM],
        out_specs=(ANY, VMEM, VMEM, VMEM),
        scratch_shapes=[
            pltpu.VMEM((PROBES, 256), jnp.float32),
            pltpu.VMEM((4, ROWS, 128), jnp.float32),
            pltpu.SemaphoreType.DMA,
        ],
        compiler_params=pltpu.CompilerParams(vmem_limit_bytes=12 * MIB),
        cost_estimate=pl.CostEstimate(
            flops=2 * PROBES * LAYERS * D * COLS, bytes_accessed=22 * MIB, transcendentals=0
        ),
        name="sketch",
    )(layer_order, arrived, probes)


def local(branch_weights, branch_gains, column_order, layer_order, probe_seeds):
    gains = lax.all_to_all(
        jnp.broadcast_to(branch_gains[None], (8, 1, ROWS)), "expert", 0, 0, tiled=True
    ).reshape(8, ROWS)
    raw = gather(column_order[0], branch_weights[0])
    blocks = fold(raw, gains, branch_gains)
    blocks, seeds = lax.optimization_barrier((blocks, probe_seeds))
    arrived = lax.all_to_all(blocks, STACK, 0, 0, tiled=True)
    probes = make_probes(layer_order, seeds)
    ordered, sums, printed, shared = sketch(layer_order, arrived, probes)
    return (
        ordered.reshape(1, LAYERS * D, COLS),
        sums[None],
        printed.reshape(1, PROBES),
        shared.reshape(LAYERS * D),
    )


def solution(mesh):
    return jax.shard_map(
        local,
        mesh=mesh,
        in_specs=(
            P("expert", STACK, None),
            P("expert", STACK),
            P("expert", None),
            P(),
            P(),
        ),
        out_specs=(
            P("expert", None, STACK),
            P("expert", None, STACK),
            P("expert", None),
            P(),
        ),
        check_vma=False,
    )
```

```python
import functools

import jax
import jax.numpy as jnp
import numpy as np
from jax import lax
from jax.experimental import pallas as pl
from jax.experimental.pallas import tpu as pltpu
from jax.sharding import PartitionSpec as P

D = 2048
FF = 8192
LAYERS = 4
PROBES = 1024
ROWS = 128
COLS = 128
GROUPS = 64
SENT = ROWS + 8
PRIME = 65521
STACK = ("section", "tensor")
MIB = 1 << 20

VMEM = pl.BlockSpec(memory_space=pltpu.VMEM)
SMEM = pl.BlockSpec(memory_space=pltpu.SMEM)
ANY = pl.BlockSpec(memory_space=pl.ANY)


def column_probe():
    hashed = (7919 * (np.arange(FF, dtype=np.int64) + 1)) % PRIME
    return ((hashed % 511 - 255) / 256.0).astype(np.float32).reshape(GROUPS, COLS)


def gather_kernel(packed_ref, w_ref, out_ref, pairs, turned, held, sem, out_sem):
    half = GROUPS // 2
    copy = pltpu.make_async_copy(packed_ref, pairs, sem)
    copy.start()

    def turn(s, _):
        at = pl.multiple_of(s * 128, 128)
        turned[pl.ds(at, 128), :] = w_ref[:, pl.ds(at, 128)].T.astype(jnp.float32)
        return 0

    lax.fori_loop(0, FF // 128, turn, 0, unroll=16)
    copy.wait()
    sublane = lax.broadcasted_iota(jnp.int32, (8, 128), 0)
    masks = [sublane == i for i in range(8)]

    def send(at, count):
        return pltpu.make_async_copy(
            held.at[pl.ds(at, count)], out_ref.at[pl.ds(at, count)], out_sem
        )

    def both(p):
        tiles = ([], [])
        for j in range(0, COLS, 8):
            made = [None, None]
            for i in range(8):
                word = pairs[p, j + i]
                for u, column in enumerate((word & 65535, lax.shift_right_logical(word, 16))):
                    row = turned[pl.ds(column, 8, stride=0), :]
                    made[u] = row if i == 0 else jnp.where(masks[i], row, made[u])
            for u in range(2):
                tiles[u].append(made[u])
        for u in range(2):
            held[p + half * u] = jnp.concatenate(tiles[u], axis=0).astype(jnp.bfloat16).T

    def step(s, _):
        for q in range(8):
            both(s * 8 + q)
        send(s * 8, 8).start()
        send(s * 8 + half, 8).start()
        return 0

    lax.fori_loop(0, half // 8, step, 0)
    send(0, GROUPS).wait()


def gather(order, weights):
    order = order.reshape(2, GROUPS // 2, COLS)
    packed = order[0] + order[1] * 65536
    return pl.pallas_call(
        gather_kernel,
        out_shape=jax.ShapeDtypeStruct((GROUPS, ROWS, COLS), jnp.bfloat16),
        in_specs=[VMEM, VMEM],
        out_specs=ANY,
        scratch_shapes=[
            pltpu.SMEM((GROUPS // 2, COLS), jnp.int32),
            pltpu.VMEM((FF, ROWS), jnp.float32),
            pltpu.VMEM((GROUPS, ROWS, COLS), jnp.bfloat16),
            pltpu.SemaphoreType.DMA,
            pltpu.SemaphoreType.DMA,
        ],
        compiler_params=pltpu.CompilerParams(vmem_limit_bytes=12 * MIB),
        cost_estimate=pl.CostEstimate(flops=0, bytes_accessed=24 * MIB, transcendentals=0),
        name="gather",
    )(packed, weights)


def pieces(value):
    high = value.astype(jnp.bfloat16).astype(jnp.float32)
    rest = value - high
    middle = rest.astype(jnp.bfloat16).astype(jnp.float32)
    return [high, middle, rest - middle]


def fold_kernel(raw_ref, gains_ref, own_ref, probe_ref, out_ref, held, extra, sem):
    mean = jnp.sum(gains_ref[...], axis=0, keepdims=True) * (1.0 / 8.0)
    scale = jnp.broadcast_to(own_ref[...] / mean, (COLS, ROWS)).T
    parts, count = 4, GROUPS // 4

    def send(c):
        return pltpu.make_async_copy(
            held.at[pl.ds(c * count, count)],
            out_ref.at[pl.ds(c * count, count), pl.ds(0, ROWS), :],
            sem.at[c],
        )

    total = jnp.zeros((ROWS, COLS), jnp.float32)
    for c in range(parts):

        def step(s, total):
            d = c * count + s
            folded = (raw_ref[d].astype(jnp.float32) * scale).astype(jnp.bfloat16)
            held[d] = folded
            return total + folded.astype(jnp.float32) * probe_ref[pl.ds(d, 1), :]

        total = lax.fori_loop(0, count, step, total, unroll=4)
        send(c).start()
    printed = jnp.sum(total.T, axis=0, keepdims=True)
    rows = pieces(printed) + pieces(mean) + [jnp.zeros((2, ROWS), jnp.float32)]
    rows = jnp.concatenate(rows, axis=0).astype(jnp.bfloat16)
    extra[...] = jnp.broadcast_to(rows[None], extra.shape)
    copy = pltpu.make_async_copy(extra, out_ref.at[:, pl.ds(ROWS, SENT - ROWS), :], sem.at[parts])
    copy.start()
    for c in range(parts):
        send(c).wait()
    copy.wait()


def fold(raw, gains, own):
    return pl.pallas_call(
        fold_kernel,
        out_shape=jax.ShapeDtypeStruct((GROUPS, SENT, COLS), jnp.bfloat16),
        in_specs=[VMEM, VMEM, VMEM, VMEM],
        out_specs=ANY,
        scratch_shapes=[
            pltpu.VMEM((GROUPS, ROWS, COLS), jnp.bfloat16),
            pltpu.VMEM((GROUPS, SENT - ROWS, COLS), jnp.bfloat16),
            pltpu.SemaphoreType.DMA((5,)),
        ],
        compiler_params=pltpu.CompilerParams(vmem_limit_bytes=8 * MIB),
        cost_estimate=pl.CostEstimate(flops=0, bytes_accessed=5 * MIB, transcendentals=0),
        name="fold",
    )(raw, gains, own, column_probe())


def reduced(value):
    left = value - (value.astype(jnp.float32) * (1.0 / PRIME)).astype(jnp.int32) * PRIME
    left = jnp.where(left < 0, left + PRIME, left)
    return jnp.where(left >= PRIME, left - PRIME, left)


def probes_kernel(layer_ref, seeds_ref, out_ref):
    lane = lax.broadcasted_iota(jnp.int32, (8, 128), 1)

    def rows(j, _):
        at = pl.multiple_of(j * 16, 16)
        seeds = [jnp.broadcast_to(seeds_ref[pl.ds(at + 8 * u, 8), :], (8, 128)) for u in range(2)]
        steps = [reduced(seed * 128) for seed in seeds]
        for b in range(LAYERS):
            hashed = [reduced(seed * (layer_ref[b] * D + 1 + lane)) for seed in seeds]
            for c in range(0, D, 128):
                made = []
                for u in range(2):
                    value = hashed[u]
                    small = lax.shift_right_logical(value, 9) + (value & 511)
                    small = jnp.where(small >= 511, small - (511 + 255), small - 255)
                    made.append(small.astype(jnp.float32) * (1.0 / 256.0))
                    after = value + steps[u] - PRIME
                    hashed[u] = jnp.where(after < 0, after + PRIME, after)
                out_ref[pl.ds(at, 16), b * D + c : b * D + c + 128] = jnp.concatenate(
                    made, axis=0
                ).astype(jnp.bfloat16)
        return 0

    lax.fori_loop(0, out_ref.shape[0] // 16, rows, 0)


def make_probes(layer_order, seeds):
    rows = PROBES // 8
    return pl.pallas_call(
        probes_kernel,
        out_shape=jax.ShapeDtypeStruct((PROBES, LAYERS * D), jnp.bfloat16),
        grid_spec=pltpu.PrefetchScalarGridSpec(
            num_scalar_prefetch=1,
            grid=(8,),
            in_specs=[pl.BlockSpec((rows, 1), lambda j, order: (j, 0))],
            out_specs=pl.BlockSpec((rows, LAYERS * D), lambda j, order: (j, 0)),
        ),
        compiler_params=pltpu.CompilerParams(vmem_limit_bytes=56 * MIB),
        cost_estimate=pl.CostEstimate(flops=0, bytes_accessed=64 * MIB, transcendentals=0),
        name="probes",
    )(layer_order, seeds.reshape(PROBES, 1))


def sketch_kernel(
    layer_ref, in_ref, probes_ref, out_ref, sums_ref, print_ref, gain_ref, total, turned, sem
):
    per_layer = GROUPS // LAYERS

    def placed(b):
        return pltpu.make_async_copy(
            in_ref.at[pl.ds(per_layer * b, per_layer), pl.ds(0, ROWS), :],
            out_ref.at[pl.ds(layer_ref[b] * per_layer, per_layer)],
            sem,
        )

    for b in range(LAYERS):
        placed(b).start()
    extra = in_ref[:, ROWS:SENT, :].astype(jnp.float32)
    mean = extra[:, 3, :] + extra[:, 4, :] + extra[:, 5, :]
    for b in range(LAYERS):
        at = pl.multiple_of(layer_ref[b] * per_layer, per_layer)
        gain_ref[pl.ds(at, per_layer), :] = mean[per_layer * b : per_layer * (b + 1)]
    row = lax.broadcasted_iota(jnp.int32, extra.shape, 1)
    printed = jnp.where(row < 3, extra, 0.0).reshape(GROUPS * 8, ROWS)
    for j in range(4):
        turned[j] = printed[j * 128 : (j + 1) * 128].T
    lane = lax.broadcasted_iota(jnp.int32, (ROWS, 128), 1) // 8

    for b in range(LAYERS):
        blocks = []
        for g in range(per_layer):
            beside = jnp.where(lane == g, turned[b], 0.0).astype(jnp.bfloat16)
            blocks.append(jnp.concatenate([in_ref[b * per_layer + g, 0:ROWS, :], beside], axis=1))
        product = jnp.dot(
            probes_ref[:, b * D : (b + 1) * D],
            jnp.concatenate(blocks, axis=0),
            preferred_element_type=jnp.float32,
        )
        if b == 0:
            total[...] = product
        else:
            total[...] += product
    sums_ref[...] = total[:, 0:COLS]
    for j in range(PROBES // 128):
        part = total[j * 128 : (j + 1) * 128, COLS:].T
        print_ref[:, j * 128 : (j + 1) * 128] = jnp.sum(part, axis=0, keepdims=True) * FF ** (-0.5)
    for b in range(LAYERS):
        placed(b).wait()


def sketch(layer_order, arrived, probes):
    return pl.pallas_call(
        sketch_kernel,
        out_shape=(
            jax.ShapeDtypeStruct((GROUPS, ROWS, COLS), jnp.bfloat16),
            jax.ShapeDtypeStruct((PROBES, COLS), jnp.float32),
            jax.ShapeDtypeStruct((1, PROBES), jnp.float32),
            jax.ShapeDtypeStruct((GROUPS, ROWS), jnp.float32),
        ),
        in_specs=[SMEM, VMEM, VMEM],
        out_specs=(ANY, VMEM, VMEM, VMEM),
        scratch_shapes=[
            pltpu.VMEM((PROBES, 256), jnp.float32),
            pltpu.VMEM((4, ROWS, 128), jnp.float32),
            pltpu.SemaphoreType.DMA,
        ],
        compiler_params=pltpu.CompilerParams(vmem_limit_bytes=12 * MIB),
        cost_estimate=pl.CostEstimate(
            flops=2 * PROBES * LAYERS * D * COLS, bytes_accessed=22 * MIB, transcendentals=0
        ),
        name="sketch",
    )(layer_order, arrived, probes)


def local(branch_weights, branch_gains, column_order, layer_order, probe_seeds):
    gains = lax.all_to_all(
        jnp.broadcast_to(branch_gains[None], (8, 1, ROWS)), "expert", 0, 0, tiled=True
    ).reshape(8, ROWS)
    raw = gather(column_order[0], branch_weights[0])
    blocks = fold(raw, gains, branch_gains)
    blocks, seeds = lax.optimization_barrier((blocks, probe_seeds))
    arrived = lax.all_to_all(blocks, STACK, 0, 0, tiled=True)
    probes = make_probes(layer_order, seeds)
    ordered, sums, printed, shared = sketch(layer_order, arrived, probes)
    return (
        ordered.reshape(1, LAYERS * D, COLS),
        sums[None],
        printed.reshape(1, PROBES),
        shared.reshape(LAYERS * D),
    )


def solution(mesh):
    return jax.shard_map(
        local,
        mesh=mesh,
        in_specs=(
            P("expert", STACK, None),
            P("expert", STACK),
            P("expert", None),
            P(),
            P(),
        ),
        out_specs=(
            P("expert", None, STACK),
            P("expert", None, STACK),
            P("expert", None),
            P(),
        ),
        check_vma=False,
    )
```

```python
import functools

import jax
import jax.numpy as jnp
import numpy as np
from jax import lax
from jax.experimental import pallas as pl
from jax.experimental.pallas import tpu as pltpu
from jax.sharding import PartitionSpec as P

D = 2048
FF = 8192
LAYERS = 4
PROBES = 1024
ROWS = 128
COLS = 128
GROUPS = 64
SENT = ROWS + 8
PRIME = 65521
STACK = ("section", "tensor")
MIB = 1 << 20

VMEM = pl.BlockSpec(memory_space=pltpu.VMEM)
SMEM = pl.BlockSpec(memory_space=pltpu.SMEM)
ANY = pl.BlockSpec(memory_space=pl.ANY)


def column_probe():
    hashed = (7919 * (np.arange(FF, dtype=np.int64) + 1)) % PRIME
    return ((hashed % 511 - 255) / 256.0).astype(np.float32).reshape(GROUPS, COLS)


def gather_kernel(packed_ref, w_ref, out_ref, pairs, turned, sem):
    half = GROUPS // 2
    copy = pltpu.make_async_copy(packed_ref, pairs, sem)
    copy.start()

    def turn(s, _):
        at = pl.multiple_of(s * 128, 128)
        turned[pl.ds(at, 128), :] = w_ref[:, pl.ds(at, 128)].T.astype(jnp.float32)
        return 0

    lax.fori_loop(0, FF // 128, turn, 0, unroll=16)
    copy.wait()
    sublane = lax.broadcasted_iota(jnp.int32, (8, 128), 0)
    masks = [sublane == i for i in range(8)]

    def both(p):
        tiles = ([], [])
        for j in range(0, COLS, 8):
            made = [None, None]
            for i in range(8):
                word = pairs[p, j + i]
                for u, column in enumerate((word & 65535, lax.shift_right_logical(word, 16))):
                    row = turned[pl.ds(column, 8, stride=0), :]
                    made[u] = row if i == 0 else jnp.where(masks[i], row, made[u])
            for u in range(2):
                tiles[u].append(made[u])
        for u in range(2):
            out_ref[p + half * u] = jnp.concatenate(tiles[u], axis=0).astype(jnp.bfloat16).T

    def step(s, _):
        for q in range(8):
            both(s * 8 + q)
        return 0

    lax.fori_loop(0, half // 8, step, 0)


def gather(order, weights):
    order = order.reshape(2, GROUPS // 2, COLS)
    packed = order[0] + order[1] * 65536
    return pl.pallas_call(
        gather_kernel,
        out_shape=jax.ShapeDtypeStruct((GROUPS, ROWS, COLS), jnp.bfloat16),
        in_specs=[VMEM, VMEM],
        out_specs=VMEM,
        scratch_shapes=[
            pltpu.SMEM((GROUPS // 2, COLS), jnp.int32),
            pltpu.VMEM((FF, ROWS), jnp.float32),
            pltpu.SemaphoreType.DMA,
        ],
        compiler_params=pltpu.CompilerParams(vmem_limit_bytes=12 * MIB),
        cost_estimate=pl.CostEstimate(flops=0, bytes_accessed=24 * MIB, transcendentals=0),
        name="gather",
    )(packed, weights)


def pieces(value):
    high = value.astype(jnp.bfloat16).astype(jnp.float32)
    rest = value - high
    middle = rest.astype(jnp.bfloat16).astype(jnp.float32)
    return [high, middle, rest - middle]


def fold_kernel(raw_ref, gains_ref, own_ref, probe_ref, out_ref, held, extra, sem):
    mean = jnp.sum(gains_ref[...], axis=0, keepdims=True) * (1.0 / 8.0)
    scale = jnp.broadcast_to(own_ref[...] / mean, (COLS, ROWS)).T
    parts, count = 4, GROUPS // 4

    def send(c):
        return pltpu.make_async_copy(
            held.at[pl.ds(c * count, count)],
            out_ref.at[pl.ds(c * count, count), pl.ds(0, ROWS), :],
            sem.at[c],
        )

    total = jnp.zeros((ROWS, COLS), jnp.float32)
    for c in range(parts):

        def step(s, total):
            d = c * count + s
            folded = (raw_ref[d].astype(jnp.float32) * scale).astype(jnp.bfloat16)
            held[d] = folded
            return total + folded.astype(jnp.float32) * probe_ref[pl.ds(d, 1), :]

        total = lax.fori_loop(0, count, step, total, unroll=4)
        send(c).start()
    printed = jnp.sum(total.T, axis=0, keepdims=True)
    rows = pieces(printed) + pieces(mean) + [jnp.zeros((2, ROWS), jnp.float32)]
    rows = jnp.concatenate(rows, axis=0).astype(jnp.bfloat16)
    extra[...] = jnp.broadcast_to(rows[None], extra.shape)
    copy = pltpu.make_async_copy(extra, out_ref.at[:, pl.ds(ROWS, SENT - ROWS), :], sem.at[parts])
    copy.start()
    for c in range(parts):
        send(c).wait()
    copy.wait()


def fold(raw, gains, own):
    return pl.pallas_call(
        fold_kernel,
        out_shape=jax.ShapeDtypeStruct((GROUPS, SENT, COLS), jnp.bfloat16),
        in_specs=[VMEM, VMEM, VMEM, VMEM],
        out_specs=ANY,
        scratch_shapes=[
            pltpu.VMEM((GROUPS, ROWS, COLS), jnp.bfloat16),
            pltpu.VMEM((GROUPS, SENT - ROWS, COLS), jnp.bfloat16),
            pltpu.SemaphoreType.DMA((5,)),
        ],
        compiler_params=pltpu.CompilerParams(vmem_limit_bytes=8 * MIB),
        cost_estimate=pl.CostEstimate(flops=0, bytes_accessed=5 * MIB, transcendentals=0),
        name="fold",
    )(raw, gains, own, column_probe())


def reduced(value):
    left = value - (value.astype(jnp.float32) * (1.0 / PRIME)).astype(jnp.int32) * PRIME
    left = jnp.where(left < 0, left + PRIME, left)
    return jnp.where(left >= PRIME, left - PRIME, left)


def probes_kernel(layer_ref, seeds_ref, out_ref):
    lane = lax.broadcasted_iota(jnp.int32, (8, 128), 1)

    def rows(j, _):
        at = pl.multiple_of(j * 16, 16)
        seeds = [jnp.broadcast_to(seeds_ref[pl.ds(at + 8 * u, 8), :], (8, 128)) for u in range(2)]
        steps = [reduced(seed * 128) for seed in seeds]
        for b in range(LAYERS):
            hashed = [reduced(seed * (layer_ref[b] * D + 1 + lane)) for seed in seeds]
            for c in range(0, D, 128):
                made = []
                for u in range(2):
                    value = hashed[u]
                    small = lax.shift_right_logical(value, 9) + (value & 511)
                    small = jnp.where(small >= 511, small - (511 + 255), small - 255)
                    made.append(small.astype(jnp.float32) * (1.0 / 256.0))
                    after = value + steps[u] - PRIME
                    hashed[u] = jnp.where(after < 0, after + PRIME, after)
                out_ref[pl.ds(at, 16), b * D + c : b * D + c + 128] = jnp.concatenate(
                    made, axis=0
                ).astype(jnp.bfloat16)
        return 0

    lax.fori_loop(0, out_ref.shape[0] // 16, rows, 0)


def make_probes(layer_order, seeds):
    rows = PROBES // 8
    return pl.pallas_call(
        probes_kernel,
        out_shape=jax.ShapeDtypeStruct((PROBES, LAYERS * D), jnp.bfloat16),
        grid_spec=pltpu.PrefetchScalarGridSpec(
            num_scalar_prefetch=1,
            grid=(8,),
            in_specs=[pl.BlockSpec((rows, 1), lambda j, order: (j, 0))],
            out_specs=pl.BlockSpec((rows, LAYERS * D), lambda j, order: (j, 0)),
        ),
        compiler_params=pltpu.CompilerParams(vmem_limit_bytes=56 * MIB),
        cost_estimate=pl.CostEstimate(flops=0, bytes_accessed=64 * MIB, transcendentals=0),
        name="probes",
    )(layer_order, seeds.reshape(PROBES, 1))


def sketch_kernel(
    layer_ref, in_ref, probes_ref, out_ref, sums_ref, print_ref, gain_ref, total, turned, sem
):
    per_layer = GROUPS // LAYERS

    def placed(b):
        return pltpu.make_async_copy(
            in_ref.at[pl.ds(per_layer * b, per_layer), pl.ds(0, ROWS), :],
            out_ref.at[pl.ds(layer_ref[b] * per_layer, per_layer)],
            sem,
        )

    for b in range(LAYERS):
        placed(b).start()
    extra = in_ref[:, ROWS:SENT, :].astype(jnp.float32)
    mean = extra[:, 3, :] + extra[:, 4, :] + extra[:, 5, :]
    for b in range(LAYERS):
        at = pl.multiple_of(layer_ref[b] * per_layer, per_layer)
        gain_ref[pl.ds(at, per_layer), :] = mean[per_layer * b : per_layer * (b + 1)]
    row = lax.broadcasted_iota(jnp.int32, extra.shape, 1)
    printed = jnp.where(row < 3, extra, 0.0).reshape(GROUPS * 8, ROWS)
    for j in range(4):
        turned[j] = printed[j * 128 : (j + 1) * 128].T
    lane = lax.broadcasted_iota(jnp.int32, (ROWS, 128), 1) // 8

    for b in range(LAYERS):
        blocks = []
        for g in range(per_layer):
            beside = jnp.where(lane == g, turned[b], 0.0).astype(jnp.bfloat16)
            blocks.append(jnp.concatenate([in_ref[b * per_layer + g, 0:ROWS, :], beside], axis=1))
        product = jnp.dot(
            probes_ref[:, b * D : (b + 1) * D],
            jnp.concatenate(blocks, axis=0),
            preferred_element_type=jnp.float32,
        )
        if b == 0:
            total[...] = product
        else:
            total[...] += product
    sums_ref[...] = total[:, 0:COLS]
    for j in range(PROBES // 128):
        part = total[j * 128 : (j + 1) * 128, COLS:].T
        print_ref[:, j * 128 : (j + 1) * 128] = jnp.sum(part, axis=0, keepdims=True) * FF ** (-0.5)
    for b in range(LAYERS):
        placed(b).wait()


def sketch(layer_order, arrived, probes):
    return pl.pallas_call(
        sketch_kernel,
        out_shape=(
            jax.ShapeDtypeStruct((GROUPS, ROWS, COLS), jnp.bfloat16),
            jax.ShapeDtypeStruct((PROBES, COLS), jnp.float32),
            jax.ShapeDtypeStruct((1, PROBES), jnp.float32),
            jax.ShapeDtypeStruct((GROUPS, ROWS), jnp.float32),
        ),
        in_specs=[SMEM, VMEM, VMEM],
        out_specs=(ANY, VMEM, VMEM, VMEM),
        scratch_shapes=[
            pltpu.VMEM((PROBES, 256), jnp.float32),
            pltpu.VMEM((4, ROWS, 128), jnp.float32),
            pltpu.SemaphoreType.DMA,
        ],
        compiler_params=pltpu.CompilerParams(vmem_limit_bytes=12 * MIB),
        cost_estimate=pl.CostEstimate(
            flops=2 * PROBES * LAYERS * D * COLS, bytes_accessed=22 * MIB, transcendentals=0
        ),
        name="sketch",
    )(layer_order, arrived, probes)


def local(branch_weights, branch_gains, column_order, layer_order, probe_seeds):
    gains = lax.all_to_all(
        jnp.broadcast_to(branch_gains[None], (8, 1, ROWS)), "expert", 0, 0, tiled=True
    ).reshape(8, ROWS)
    raw = gather(column_order[0], branch_weights[0])
    blocks = fold(raw, gains, branch_gains)
    blocks, seeds = lax.optimization_barrier((blocks, probe_seeds))
    arrived = lax.all_to_all(blocks, STACK, 0, 0, tiled=True)
    probes = make_probes(layer_order, seeds)
    ordered, sums, printed, shared = sketch(layer_order, arrived, probes)
    return (
        ordered.reshape(1, LAYERS * D, COLS),
        sums[None],
        printed.reshape(1, PROBES),
        shared.reshape(LAYERS * D),
    )


def solution(mesh):
    return jax.shard_map(
        local,
        mesh=mesh,
        in_specs=(
            P("expert", STACK, None),
            P("expert", STACK),
            P("expert", None),
            P(),
            P(),
        ),
        out_specs=(
            P("expert", None, STACK),
            P("expert", None, STACK),
            P("expert", None),
            P(),
        ),
        check_vma=False,
    )
```
